32 devices in a mesh: state: 8 (over y, x, core), dp: 4 (over z).
Axes of the slice: x: 2, y: 2, z: 4, core: 2. Of those that a mesh axis runs over, the one named last changes fastest.
Arguments:
- state_ensemble: float32 [16384, 256], P('state'), may hold values from -80 to 80, as said below
- predicted_data: float32 [16384, 256], P(('state', 'dp')), may hold values from -125 to 125, as said below
- innovations: bfloat16 [16384, 256], P(('state', 'dp')), may hold values from -6 to 6
Outputs:
- increment: float32 [16384, 256], P(('state', 'dp'))
The draws below stay inside these ranges and needn't reach their ends.
Inputs may be any that keep to these rules, and one draw needn't show every extreme that they name: `state_ensemble`: finite values. `predicted_data`: finite values.
All inputs are finite; a program needn't handle non-finite values.
Results may differ from the reference program's by a relative error of at most 0.0042.
Values may be sent and summed in bfloat16 or wider, within the bound.
A program may use at most 64 MiB of HBM per device.

```python
import math
import jax
import jax.numpy as jnp
from jax import lax

NE = 256
NX = 16384
ND = 16384


def joint_draw(key):
    base = jax.random.fold_in(key, 11)
    keys = jax.random.split(base, 4)
    latent = jnp.clip(jax.random.normal(keys[0], (NX, NE), jnp.float32), -6.0, 6.0)
    first = jax.random.randint(keys[1], (ND,), 0, NX)
    second = jax.random.randint(keys[2], (ND,), 0, NX)
    noise = jnp.clip(jax.random.normal(keys[3], (ND, NE), jnp.float32), -6.0, 6.0)
    data = 0.7 * latent[first] + 0.5 * latent[second] + 0.5 * noise
    state = latent
    return (state, data)


def draw_state_ensemble(key, part):
    return joint_draw(key)[0]


def draw_predicted_data(key, part):
    return joint_draw(key)[1]


def levels(own_key, shape, cuts, least, top_value):
    def one(dim, blocks):
        heights = jax.random.uniform(jax.random.fold_in(jax.random.fold_in(own_key, 6), dim), (blocks,), jnp.float32, least / len(cuts), top_value / len(cuts))
        return jnp.repeat(jnp.exp(heights), shape[dim] // blocks).reshape((-1,) + (1,) * (len(shape) - dim - 1))

    loudness = one(*cuts[0])
    for cut in cuts[1:]:
        loudness = loudness * one(*cut)
    return loudness


def centred(stream_key, dims, scale, reach, shards=(), dtype=jnp.bfloat16):
    factor_of = levels(stream_key, dims, shards, -0.22, 0.18) if shards else 1.0
    array = jax.random.normal(stream_key, dims, jnp.float32) * scale * factor_of
    return jnp.minimum(jnp.maximum(array, -reach), reach).astype(dtype)


def setup_inputs(seed: int = 0) -> dict:
    streams_of = jax.random.split(jax.random.key(seed), 4)
    return {
        "state_ensemble": draw_state_ensemble(jax.random.fold_in(streams_of[3], 71), 0),
        "predicted_data": draw_predicted_data(jax.random.fold_in(streams_of[3], 71), 0),
        "innovations": centred(streams_of[2], (ND, NE), 1.0, 6.0, ((0, 32),)),
    }


def standardize(values):
    anomalies = values - lax.optimization_barrier(jnp.mean(values, axis=1, keepdims=True))
    spread = jnp.sqrt(lax.optimization_barrier(jnp.sum(anomalies * anomalies, axis=1)) / (NE - 1) + 1e-06)
    return ((anomalies / spread[:, None]).astype(jnp.bfloat16), spread)

def reference(state_ensemble, predicted_data, innovations):
    state_std, spread = standardize(state_ensemble)
    data_std, unused = standardize(predicted_data)
    data_size = math.gcd(ND, 512)
    state_size = math.gcd(NX, 2048)
    data_blocks = data_std.astype(jnp.float32).reshape(ND // data_size, data_size, NE)
    innov_blocks = innovations.astype(jnp.float32).reshape(ND // data_size, data_size, NE)

    def per_state(rows_block):

        def advance(running, pair):
            correl = jnp.dot(rows_block, pair[0].T) / (NE - 1)
            localized = (correl * correl * correl).astype(jnp.bfloat16).astype(jnp.float32)
            return (running + jnp.dot(localized, pair[1]), None)
        start_zero = jnp.zeros((rows_block.shape[0], NE), jnp.float32)
        return lax.scan(advance, start_zero, (data_blocks, innov_blocks))[0]
    stacked = state_std.astype(jnp.float32).reshape(NX // state_size, state_size, NE)
    summed = lax.map(per_state, stacked).reshape(NX, NE)
    return spread[:, None] * summed
```

```python
import functools

import jax
import jax.numpy as jnp
from jax import lax
from jax.experimental import pallas as pl
from jax.experimental.pallas import tpu as pltpu
from jax.sharding import PartitionSpec as P

MESH = pl.DeviceIdType.MESH
PIECES = 2


def standardize(values):
    members = values.shape[1]
    anomalies = values - jnp.mean(values, axis=1, keepdims=True)
    spread = jnp.sqrt(jnp.sum(anomalies * anomalies, axis=1, keepdims=True) / (members - 1) + 1e-06)
    return anomalies * (1.0 / spread), spread


def kernel(n_s, n_dp, state_in, data_in, innov_in, out_ref, state_raw, data_raw, sbuf, spread_buf,
           acc, dbuf, nbuf, rs_out, rs_in, local_sem, send_sem, recv_sem, rs_send_sem, rs_recv_sem):
    s = lax.axis_index("state")
    d = lax.axis_index("dp")
    rows, members = state_in.shape
    count = data_in.shape[0]
    half = count // 2
    outers = n_s // 4
    core, inner, outer = lax.rem(s, 2), lax.rem(lax.div(s, 2), 2), lax.div(s, 4)
    sib = s + 1 - 2 * core
    across = s + 2 - 4 * inner
    across_sib = sib + 2 - 4 * inner

    def other(base, k):
        return lax.rem(base + 4 * k, n_s)

    right, left = lax.rem(d + 1, n_dp), lax.rem(d + n_dp - 1, n_dp)

    load_data = [
        pltpu.make_async_copy(
            data_in.at[pl.ds(h * half, half)], data_raw.at[pl.ds(h * half, half)], local_sem.at[h])
        for h in range(2)
    ]
    load_innov = [
        pltpu.make_async_copy(
            innov_in.at[pl.ds(h * half, half)], nbuf.at[s, h], local_sem.at[2 + h])
        for h in range(2)
    ]
    load_state = pltpu.make_async_copy(state_in, state_raw, local_sem.at[4])
    for h in (1, 0):
        load_data[h].start()
    load_state.start()
    for h in range(2):
        load_innov[h].start()

    barrier = pltpu.get_barrier_semaphore()
    partners = [sib, across] + [other(s, k) for k in range(1, outers)]
    for p in partners:
        pl.semaphore_signal(barrier, inc=1, device_id={"state": p}, device_id_type=MESH)
    for p in (right, left):
        pl.semaphore_signal(barrier, inc=1, device_id={"dp": p}, device_id_type=MESH)
    pl.semaphore_wait(barrier, len(partners) + 2)

    sends = []

    def send(array, owner, h, dest, src=None):
        buf = (dbuf, nbuf)[array]
        copy = pltpu.make_async_remote_copy(
            src_ref=buf.at[owner, h] if src is None else src,
            dst_ref=buf.at[owner, h],
            send_sem=send_sem.at[len(sends)],
            recv_sem=recv_sem.at[array, owner, h],
            device_id={"state": dest},
            device_id_type=MESH,
        )
        copy.start()
        sends.append(copy)

    def arrived(array, owner, h):
        buf = (dbuf, nbuf)[array]
        pltpu.make_async_remote_copy(
            src_ref=buf.at[owner, h],
            dst_ref=buf.at[owner, h],
            send_sem=send_sem.at[0],
            recv_sem=recv_sem.at[array, owner, h],
            device_id={"state": across},
            device_id_type=MESH,
        ).wait_recv()

    outer_ks = list(range(1, outers))

    def send_innov(h, dests):
        for dest in dests:
            send(1, s, h, dest, src=innov_in.at[pl.ds(h * half, half)])

    outer_devs = [other(s, k) for k in outer_ks]
    send_innov(1, [across])
    send_innov(0, outer_devs + [sib])

    for h in (1, 0):
        load_data[h].wait()
        std, _ = standardize(data_raw[pl.ds(h * half, half), :])
        dbuf[s, h] = std.T.astype(jnp.bfloat16)
    send(0, s, 1, across)
    for dest in outer_devs:
        send(0, s, 0, dest)
    send(0, s, 0, sib)
    send_innov(0, [across])
    send_innov(1, outer_devs + [sib])
    send(0, s, 0, across)
    for dest in outer_devs:
        send(0, s, 1, dest)
    send(0, s, 1, sib)

    load_state.wait()
    tile = rows // 8

    def state_tile(j, carry):
        at = pl.ds(pl.multiple_of(j * tile, tile), tile)
        std, spread = standardize(state_raw[at, :])
        sbuf[at, :] = std.astype(jnp.bfloat16)
        spread_buf[at, :] = spread
        return carry

    lax.fori_loop(0, 8, state_tile, 0)

    def partial(at, units):
        x = sbuf[at, :]
        total = None
        for owner, h in units:
            correl = jnp.dot(x, dbuf[owner, h], preferred_element_type=jnp.float32)
            localized = (correl * correl * correl).astype(jnp.bfloat16)
            term = jnp.dot(localized, nbuf[owner, h], preferred_element_type=jnp.float32)
            total = term if total is None else total + term
        return total

    def compute(units, first=False):
        def step(j, carry):
            at = pl.ds(pl.multiple_of(j * tile, tile), tile)
            total = partial(at, units)
            acc[at, :] = total if first else acc[at, :] + total
            return carry

        lax.fori_loop(0, 8, step, 0)

    def both(owner, h):
        arrived(1, owner, h)
        arrived(0, owner, h)

    def take(owner, h, onward):
        for array in (1, 0):
            arrived(array, owner, h)
            for dest in onward:
                send(array, owner, h, dest)

    for h in range(2):
        load_innov[h].wait()
    compute([(s, 0), (s, 1)], first=True)
    both(sib, 0)
    both(sib, 1)
    compute([(sib, 0), (sib, 1)])

    take(across, 1, outer_devs + [sib])
    for k in outer_ks:
        take(other(s, k), 0, [across, sib])
    compute([(across, 1)] + [(other(s, k), 0) for k in outer_ks])
    both(across_sib, 1)
    for k in outer_ks:
        both(other(sib, k), 0)
    take(across, 0, [sib])
    for k in outer_ks:
        take(other(s, k), 1, [sib])
    compute([(across_sib, 1)] + [(other(sib, k), 0) for k in outer_ks])
    compute([(across, 0)] + [(other(s, k), 1) for k in outer_ks])
    both(across_sib, 0)
    for k in outer_ks:
        both(other(sib, k), 1)
    compute([(across_sib, 0)] + [(other(sib, k), 1) for k in outer_ks])

    last_units = []
    for k in outer_ks:
        own_plane, sib_plane = other(across, k), other(across_sib, k)
        for h in range(2):
            take(own_plane, h, [sib])
        if k < outers - 1:
            compute([(own_plane, 0), (own_plane, 1)])
        for h in range(2):
            both(sib_plane, h)
        if k < outers - 1:
            compute([(sib_plane, 0), (sib_plane, 1)])
        else:
            last_units = [(own_plane, 0), (own_plane, 1), (sib_plane, 0), (sib_plane, 1)]

    target_rows = rows // n_dp
    ring_rows = target_rows // 2
    piece = ring_rows // PIECES
    scale = 1.0 / float(members - 1) ** 3

    def rs_copy(way, step, p):
        return pltpu.make_async_remote_copy(
            src_ref=rs_out.at[way, step, p],
            dst_ref=rs_in.at[way, step, p],
            send_sem=rs_send_sem.at[way, step, p],
            recv_sem=rs_recv_sem.at[way, step, p],
            device_id={"dp": (right, left)[way]},
            device_id_type=MESH,
        )

    for step in range(n_dp):
        for way in range(2):
            target = lax.rem(d + (n_dp - 1 - step if way == 0 else 1 + step), n_dp)
            base = target * target_rows + way * ring_rows
            at = pl.ds(pl.multiple_of(base, ring_rows), ring_rows)
            acc[at, :] += partial(at, last_units)
        for p in range(PIECES):
            for way in range(2):
                target = lax.rem(d + (n_dp - 1 - step if way == 0 else 1 + step), n_dp)
                base = target * target_rows + way * ring_rows + p * piece
                at = pl.ds(pl.multiple_of(base, piece), piece)
                value = acc[at, :]
                if step > 0:
                    rs_copy(way, step - 1, p).wait_recv()
                    value = value + rs_in[way, step - 1, p].astype(jnp.float32)
                if step < n_dp - 1:
                    rs_out[way, step, p] = value.astype(jnp.bfloat16)
                    rs_copy(way, step, p).start()
                else:
                    out_ref[pl.ds(way * ring_rows + p * piece, piece), :] = (
                        value * (spread_buf[at, :] * scale))

    for copy in sends:
        copy.wait_send()
    for step in range(n_dp - 1):
        for way in range(2):
            for p in range(PIECES):
                rs_copy(way, step, p).wait_send()


def on_device(n_s, n_dp, state_ensemble, predicted_data, innovations):
    rows, members = state_ensemble.shape
    count = predicted_data.shape[0]
    half = count // 2
    outers = n_s // 4
    n_sends = 4 * (n_s // 2) + 4 + 2 * (outers - 1) + 6 * (outers - 1)
    ring = (2, n_dp - 1, PIECES, rows // n_dp // 2 // PIECES, members)
    any_spec = pl.BlockSpec(memory_space=pl.ANY)
    return pl.pallas_call(
        functools.partial(kernel, n_s, n_dp),
        out_shape=jax.ShapeDtypeStruct((rows // n_dp, members), jnp.float32),
        in_specs=[any_spec] * 3,
        out_specs=pl.BlockSpec(memory_space=pltpu.VMEM),
        scratch_shapes=[
            pltpu.VMEM((rows, members), jnp.float32),
            pltpu.VMEM((count, members), jnp.float32),
            pltpu.VMEM((rows, members), jnp.bfloat16),
            pltpu.VMEM((rows, 1), jnp.float32),
            pltpu.VMEM((rows, members), jnp.float32),
            pltpu.VMEM((n_s, 2, members, half), jnp.bfloat16),
            pltpu.VMEM((n_s, 2, half, members), jnp.bfloat16),
            pltpu.VMEM(ring, jnp.bfloat16),
            pltpu.VMEM(ring, jnp.bfloat16),
            pltpu.SemaphoreType.DMA((5,)),
            pltpu.SemaphoreType.DMA((n_sends,)),
            pltpu.SemaphoreType.DMA((2, n_s, 2)),
            pltpu.SemaphoreType.DMA(ring[:3]),
            pltpu.SemaphoreType.DMA(ring[:3]),
        ],
        compiler_params=pltpu.CompilerParams(
            collective_id=0, has_side_effects=True, vmem_limit_bytes=48 * 1024 * 1024),
    )(state_ensemble, predicted_data, innovations)


def solution(mesh):
    in_specs = (P("state", None), P(("state", "dp"), None), P(("state", "dp"), None))
    out_specs = P(("state", "dp"), None)
    body = functools.partial(on_device, mesh.shape["state"], mesh.shape["dp"])
    return jax.shard_map(
        body, mesh=mesh, in_specs=in_specs, out_specs=out_specs, check_vma=False
    )
```

```python
import functools

import jax
import jax.numpy as jnp
from jax import lax
from jax.experimental import pallas as pl
from jax.experimental.pallas import tpu as pltpu
from jax.sharding import PartitionSpec as P

MESH = pl.DeviceIdType.MESH
WIDE_STEPS = 2
PIECES = 2


def standardize(values):
    members = values.shape[1]
    anomalies = values - jnp.mean(values, axis=1, keepdims=True)
    spread = jnp.sqrt(jnp.sum(anomalies * anomalies, axis=1, keepdims=True) / (members - 1) + 1e-06)
    return anomalies * (1.0 / spread), spread


def kernel(n_s, n_dp, state_in, data_in, innov_in, out_ref, state_raw, data_raw, sbuf, spread_buf,
           acc, dbuf, nbuf, rs_out, rs_in, local_sem, send_sem, recv_sem, rs_send_sem, rs_recv_sem):
    s = lax.axis_index("state")
    d = lax.axis_index("dp")
    rows, members = state_in.shape
    count = data_in.shape[0]
    half = count // 2
    outers = n_s // 4
    core, inner, outer = lax.rem(s, 2), lax.rem(lax.div(s, 2), 2), lax.div(s, 4)
    sib = s + 1 - 2 * core
    across = s + 2 - 4 * inner
    across_sib = sib + 2 - 4 * inner

    def other(base, k):
        return lax.rem(base + 4 * k, n_s)

    right, left = lax.rem(d + 1, n_dp), lax.rem(d + n_dp - 1, n_dp)

    load_data = [
        pltpu.make_async_copy(
            data_in.at[pl.ds(h * half, half)], data_raw.at[pl.ds(h * half, half)], local_sem.at[h])
        for h in range(2)
    ]
    load_innov = [
        pltpu.make_async_copy(
            innov_in.at[pl.ds(h * half, half)], nbuf.at[s, h], local_sem.at[2 + h])
        for h in range(2)
    ]
    load_state = pltpu.make_async_copy(state_in, state_raw, local_sem.at[4])
    for h in (1, 0):
        load_data[h].start()
    load_state.start()
    for h in range(2):
        load_innov[h].start()

    barrier = pltpu.get_barrier_semaphore()
    partners = [sib, across] + [other(s, k) for k in range(1, outers)]
    for p in partners:
        pl.semaphore_signal(barrier, inc=1, device_id={"state": p}, device_id_type=MESH)
    for p in (right, left):
        pl.semaphore_signal(barrier, inc=1, device_id={"dp": p}, device_id_type=MESH)
    pl.semaphore_wait(barrier, len(partners) + 2)

    sends = []

    def send(array, owner, h, dest, src=None):
        buf = (dbuf, nbuf)[array]
        copy = pltpu.make_async_remote_copy(
            src_ref=buf.at[owner, h] if src is None else src,
            dst_ref=buf.at[owner, h],
            send_sem=send_sem.at[len(sends)],
            recv_sem=recv_sem.at[array, owner, h],
            device_id={"state": dest},
            device_id_type=MESH,
        )
        copy.start()
        sends.append(copy)

    def arrived(array, owner, h):
        buf = (dbuf, nbuf)[array]
        pltpu.make_async_remote_copy(
            src_ref=buf.at[owner, h],
            dst_ref=buf.at[owner, h],
            send_sem=send_sem.at[0],
            recv_sem=recv_sem.at[array, owner, h],
            device_id={"state": across},
            device_id_type=MESH,
        ).wait_recv()

    outer_ks = list(range(1, outers))

    def send_innov(h, dests):
        for dest in dests:
            send(1, s, h, dest, src=innov_in.at[pl.ds(h * half, half)])

    outer_devs = [other(s, k) for k in outer_ks]
    send_innov(1, [across])
    send_innov(0, outer_devs + [sib])

    for h in (1, 0):
        load_data[h].wait()
        std, _ = standardize(data_raw[pl.ds(h * half, half), :])
        dbuf[s, h] = std.T.astype(jnp.bfloat16)
    send(0, s, 1, across)
    for dest in outer_devs:
        send(0, s, 0, dest)
    send(0, s, 0, sib)
    send_innov(0, [across])
    send_innov(1, outer_devs + [sib])
    send(0, s, 0, across)
    for dest in outer_devs:
        send(0, s, 1, dest)
    send(0, s, 1, sib)

    load_state.wait()
    tile = rows // 8
    wide = rows // WIDE_STEPS

    def state_tile(j, carry):
        at = pl.ds(pl.multiple_of(j * tile, tile), tile)
        std, spread = standardize(state_raw[at, :])
        sbuf[at, :] = std.astype(jnp.bfloat16)
        spread_buf[at, :] = spread
        return carry

    lax.fori_loop(0, 8, state_tile, 0)

    def partial(x, units):
        total = None
        for owner, h in units:
            correl = jnp.dot(x, dbuf[owner, h], preferred_element_type=jnp.float32)
            localized = (correl * correl * correl).astype(jnp.bfloat16)
            term = jnp.dot(localized, nbuf[owner, h], preferred_element_type=jnp.float32)
            total = term if total is None else total + term
        return total

    def compute(units, first=False):
        def step(j, carry):
            at = pl.ds(pl.multiple_of(j * wide, wide), wide)
            total = partial(sbuf[at, :], units)
            acc[at, :] = total if first else acc[at, :] + total
            return carry

        lax.fori_loop(0, WIDE_STEPS, step, 0)

    def both(owner, h):
        arrived(1, owner, h)
        arrived(0, owner, h)

    def take(owner, h, onward):
        for array in (1, 0):
            arrived(array, owner, h)
            for dest in onward:
                send(array, owner, h, dest)

    for h in range(2):
        load_innov[h].wait()
    compute([(s, 0), (s, 1)], first=True)
    both(sib, 0)
    both(sib, 1)
    compute([(sib, 0), (sib, 1)])

    take(across, 1, outer_devs + [sib])
    for k in outer_ks:
        take(other(s, k), 0, [across, sib])
    compute([(across, 1)] + [(other(s, k), 0) for k in outer_ks])
    both(across_sib, 1)
    for k in outer_ks:
        both(other(sib, k), 0)
    take(across, 0, [sib])
    for k in outer_ks:
        take(other(s, k), 1, [sib])
    compute([(across_sib, 1)] + [(other(sib, k), 0) for k in outer_ks])
    compute([(across, 0)] + [(other(s, k), 1) for k in outer_ks])
    both(across_sib, 0)
    for k in outer_ks:
        both(other(sib, k), 1)
    compute([(across_sib, 0)] + [(other(sib, k), 1) for k in outer_ks])

    last_units = []
    for k in outer_ks:
        own_plane, sib_plane = other(across, k), other(across_sib, k)
        for h in range(2):
            take(own_plane, h, [sib])
        if k < outers - 1:
            compute([(own_plane, 0), (own_plane, 1)])
        for h in range(2):
            both(sib_plane, h)
        if k < outers - 1:
            compute([(sib_plane, 0), (sib_plane, 1)])
        else:
            last_units = [(own_plane, 0), (own_plane, 1), (sib_plane, 0), (sib_plane, 1)]

    target_rows = rows // n_dp
    ring_rows = target_rows // 2
    piece = ring_rows // PIECES
    scale = 1.0 / float(members - 1) ** 3

    def rs_copy(way, step, p):
        return pltpu.make_async_remote_copy(
            src_ref=rs_out.at[way, step, p],
            dst_ref=rs_in.at[way, step, p],
            send_sem=rs_send_sem.at[way, step, p],
            recv_sem=rs_recv_sem.at[way, step, p],
            device_id={"dp": (right, left)[way]},
            device_id_type=MESH,
        )

    for step in range(n_dp):
        ats = []
        for way in range(2):
            target = lax.rem(d + (n_dp - 1 - step if way == 0 else 1 + step), n_dp)
            base = target * target_rows + way * ring_rows
            ats.append(pl.ds(pl.multiple_of(base, ring_rows), ring_rows))
        total = partial(jnp.concatenate([sbuf[at, :] for at in ats], axis=0), last_units)
        for way in range(2):
            acc[ats[way], :] += total[way * ring_rows:(way + 1) * ring_rows]
        for p in range(PIECES):
            for way in range(2):
                target = lax.rem(d + (n_dp - 1 - step if way == 0 else 1 + step), n_dp)
                base = target * target_rows + way * ring_rows + p * piece
                at = pl.ds(pl.multiple_of(base, piece), piece)
                value = acc[at, :]
                if step > 0:
                    rs_copy(way, step - 1, p).wait_recv()
                    value = value + rs_in[way, step - 1, p].astype(jnp.float32)
                if step < n_dp - 1:
                    rs_out[way, step, p] = value.astype(jnp.bfloat16)
                    rs_copy(way, step, p).start()
                else:
                    out_ref[pl.ds(way * ring_rows + p * piece, piece), :] = (
                        value * (spread_buf[at, :] * scale))

    for copy in sends:
        copy.wait_send()
    for step in range(n_dp - 1):
        for way in range(2):
            for p in range(PIECES):
                rs_copy(way, step, p).wait_send()


def on_device(n_s, n_dp, state_ensemble, predicted_data, innovations):
    rows, members = state_ensemble.shape
    count = predicted_data.shape[0]
    half = count // 2
    outers = n_s // 4
    n_sends = 4 * (n_s // 2) + 4 + 2 * (outers - 1) + 6 * (outers - 1)
    ring = (2, n_dp - 1, PIECES, rows // n_dp // 2 // PIECES, members)
    any_spec = pl.BlockSpec(memory_space=pltpu.HBM)
    return pl.pallas_call(
        functools.partial(kernel, n_s, n_dp),
        out_shape=jax.ShapeDtypeStruct((rows // n_dp, members), jnp.float32),
        in_specs=[any_spec] * 3,
        out_specs=pl.BlockSpec(memory_space=pltpu.VMEM),
        scratch_shapes=[
            pltpu.VMEM((rows, members), jnp.float32),
            pltpu.VMEM((count, members), jnp.float32),
            pltpu.VMEM((rows, members), jnp.bfloat16),
            pltpu.VMEM((rows, 1), jnp.float32),
            pltpu.VMEM((rows, members), jnp.float32),
            pltpu.VMEM((n_s, 2, members, half), jnp.bfloat16),
            pltpu.VMEM((n_s, 2, half, members), jnp.bfloat16),
            pltpu.VMEM(ring, jnp.bfloat16),
            pltpu.VMEM(ring, jnp.bfloat16),
            pltpu.SemaphoreType.DMA((5,)),
            pltpu.SemaphoreType.DMA((n_sends,)),
            pltpu.SemaphoreType.DMA((2, n_s, 2)),
            pltpu.SemaphoreType.DMA(ring[:3]),
            pltpu.SemaphoreType.DMA(ring[:3]),
        ],
        compiler_params=pltpu.CompilerParams(
            collective_id=0, has_side_effects=True, vmem_limit_bytes=48 * 1024 * 1024),
    )(state_ensemble, predicted_data, innovations)


def solution(mesh):
    in_specs = (P("state", None), P(("state", "dp"), None), P(("state", "dp"), None))
    out_specs = P(("state", "dp"), None)
    body = functools.partial(on_device, mesh.shape["state"], mesh.shape["dp"])
    return jax.shard_map(
        body, mesh=mesh, in_specs=in_specs, out_specs=out_specs, check_vma=False
    )
```

```python
import functools

import jax
import jax.numpy as jnp
from jax import lax
from jax.experimental import pallas as pl
from jax.experimental.pallas import tpu as pltpu
from jax.sharding import PartitionSpec as P

MESH = pl.DeviceIdType.MESH
WIDE_STEPS = 1
PIECES = 2


def standardize(values):
    members = values.shape[1]
    anomalies = values - jnp.mean(values, axis=1, keepdims=True)
    spread = jnp.sqrt(jnp.sum(anomalies * anomalies, axis=1, keepdims=True) / (members - 1) + 1e-06)
    return anomalies * (1.0 / spread), spread


def kernel(n_s, n_dp, state_in, data_in, innov_in, out_ref, state_raw, data_raw, sbuf, spread_buf,
           acc, dbuf, nbuf, rs_out, rs_in, local_sem, send_sem, recv_sem, rs_send_sem, rs_recv_sem):
    s = lax.axis_index("state")
    d = lax.axis_index("dp")
    rows, members = state_in.shape
    count = data_in.shape[0]
    half = count // 2
    outers = n_s // 4
    core, inner, outer = lax.rem(s, 2), lax.rem(lax.div(s, 2), 2), lax.div(s, 4)
    sib = s + 1 - 2 * core
    across = s + 2 - 4 * inner
    across_sib = sib + 2 - 4 * inner

    def other(base, k):
        return lax.rem(base + 4 * k, n_s)

    right, left = lax.rem(d + 1, n_dp), lax.rem(d + n_dp - 1, n_dp)

    load_data = [
        pltpu.make_async_copy(
            data_in.at[pl.ds(h * half, half)], data_raw.at[pl.ds(h * half, half)], local_sem.at[h])
        for h in range(2)
    ]
    load_innov = [
        pltpu.make_async_copy(
            innov_in.at[pl.ds(h * half, half)], nbuf.at[s, h], local_sem.at[2 + h])
        for h in range(2)
    ]
    load_state = pltpu.make_async_copy(state_in, state_raw, local_sem.at[4])
    for h in (1, 0):
        load_data[h].start()
    load_state.start()
    for h in range(2):
        load_innov[h].start()

    barrier = pltpu.get_barrier_semaphore()
    partners = [sib, across] + [other(s, k) for k in range(1, outers)]
    for p in partners:
        pl.semaphore_signal(barrier, inc=1, device_id={"state": p}, device_id_type=MESH)
    for p in (right, left):
        pl.semaphore_signal(barrier, inc=1, device_id={"dp": p}, device_id_type=MESH)
    pl.semaphore_wait(barrier, len(partners) + 2)

    sends = []

    def send(array, owner, h, dest, src=None):
        buf = (dbuf, nbuf)[array]
        copy = pltpu.make_async_remote_copy(
            src_ref=buf.at[owner, h] if src is None else src,
            dst_ref=buf.at[owner, h],
            send_sem=send_sem.at[len(sends)],
            recv_sem=recv_sem.at[array, owner, h],
            device_id={"state": dest},
            device_id_type=MESH,
        )
        copy.start()
        sends.append(copy)

    def arrived(array, owner, h):
        buf = (dbuf, nbuf)[array]
        pltpu.make_async_remote_copy(
            src_ref=buf.at[owner, h],
            dst_ref=buf.at[owner, h],
            send_sem=send_sem.at[0],
            recv_sem=recv_sem.at[array, owner, h],
            device_id={"state": across},
            device_id_type=MESH,
        ).wait_recv()

    outer_ks = list(range(1, outers))

    def send_innov(h, dests):
        for dest in dests:
            send(1, s, h, dest, src=innov_in.at[pl.ds(h * half, half)])

    outer_devs = [other(s, k) for k in outer_ks]
    send_innov(1, [across])
    send_innov(0, outer_devs + [sib])

    for h in (1, 0):
        load_data[h].wait()
        std, _ = standardize(data_raw[pl.ds(h * half, half), :])
        dbuf[s, h] = std.T.astype(jnp.bfloat16)
    send(0, s, 1, across)
    for dest in outer_devs:
        send(0, s, 0, dest)
    send(0, s, 0, sib)
    send_innov(0, [across])
    send_innov(1, outer_devs + [sib])
    send(0, s, 0, across)
    for dest in outer_devs:
        send(0, s, 1, dest)
    send(0, s, 1, sib)

    load_state.wait()
    tile = rows // 8
    wide = rows // WIDE_STEPS

    def state_tile(j, carry):
        at = pl.ds(pl.multiple_of(j * tile, tile), tile)
        std, spread = standardize(state_raw[at, :])
        sbuf[at, :] = std.astype(jnp.bfloat16)
        spread_buf[at, :] = spread
        return carry

    lax.fori_loop(0, 8, state_tile, 0)

    def partial(x, units):
        total = None
        for owner, h in units:
            correl = jnp.dot(x, dbuf[owner, h], preferred_element_type=jnp.float32)
            localized = (correl * correl * correl).astype(jnp.bfloat16)
            term = jnp.dot(localized, nbuf[owner, h], preferred_element_type=jnp.float32)
            total = term if total is None else total + term
        return total

    def compute(units, first=False):
        def step(j, carry):
            at = pl.ds(pl.multiple_of(j * wide, wide), wide)
            total = partial(sbuf[at, :], units)
            acc[at, :] = total if first else acc[at, :] + total
            return carry

        lax.fori_loop(0, WIDE_STEPS, step, 0)

    def both(owner, h):
        arrived(1, owner, h)
        arrived(0, owner, h)

    def take(owner, h, onward):
        for array in (1, 0):
            arrived(array, owner, h)
            for dest in onward:
                send(array, owner, h, dest)

    for h in range(2):
        load_innov[h].wait()
    compute([(s, 0), (s, 1)], first=True)
    both(sib, 0)
    both(sib, 1)
    compute([(sib, 0), (sib, 1)])

    take(across, 1, outer_devs + [sib])
    for k in outer_ks:
        take(other(s, k), 0, [across, sib])
    compute([(across, 1)] + [(other(s, k), 0) for k in outer_ks])
    both(across_sib, 1)
    for k in outer_ks:
        both(other(sib, k), 0)
    take(across, 0, [sib])
    for k in outer_ks:
        take(other(s, k), 1, [sib])
    compute([(across_sib, 1)] + [(other(sib, k), 0) for k in outer_ks])
    compute([(across, 0)] + [(other(s, k), 1) for k in outer_ks])
    both(across_sib, 0)
    for k in outer_ks:
        both(other(sib, k), 1)
    compute([(across_sib, 0)] + [(other(sib, k), 1) for k in outer_ks])

    last_units = []
    for k in outer_ks:
        own_plane, sib_plane = other(across, k), other(across_sib, k)
        for h in range(2):
            take(own_plane, h, [sib])
        if k < outers - 1:
            compute([(own_plane, 0), (own_plane, 1)])
        for h in range(2):
            both(sib_plane, h)
        if k < outers - 1:
            compute([(sib_plane, 0), (sib_plane, 1)])
        else:
            last_units = [(own_plane, 0), (own_plane, 1), (sib_plane, 0), (sib_plane, 1)]

    target_rows = rows // n_dp
    ring_rows = target_rows // 2
    piece = ring_rows // PIECES
    scale = 1.0 / float(members - 1) ** 3

    def rs_copy(way, step, p):
        return pltpu.make_async_remote_copy(
            src_ref=rs_out.at[way, step, p],
            dst_ref=rs_in.at[way, step, p],
            send_sem=rs_send_sem.at[way, step, p],
            recv_sem=rs_recv_sem.at[way, step, p],
            device_id={"dp": (right, left)[way]},
            device_id_type=MESH,
        )

    for step in range(n_dp):
        ats = []
        for way in range(2):
            target = lax.rem(d + (n_dp - 1 - step if way == 0 else 1 + step), n_dp)
            base = target * target_rows + way * ring_rows
            ats.append(pl.ds(pl.multiple_of(base, ring_rows), ring_rows))
        total = partial(jnp.concatenate([sbuf[at, :] for at in ats], axis=0), last_units)
        for way in range(2):
            acc[ats[way], :] += total[way * ring_rows:(way + 1) * ring_rows]
        for p in range(PIECES):
            for way in range(2):
                target = lax.rem(d + (n_dp - 1 - step if way == 0 else 1 + step), n_dp)
                base = target * target_rows + way * ring_rows + p * piece
                at = pl.ds(pl.multiple_of(base, piece), piece)
                value = acc[at, :]
                if step > 0:
                    rs_copy(way, step - 1, p).wait_recv()
                    value = value + rs_in[way, step - 1, p].astype(jnp.float32)
                if step < n_dp - 1:
                    rs_out[way, step, p] = value.astype(jnp.bfloat16)
                    rs_copy(way, step, p).start()
                else:
                    out_ref[pl.ds(way * ring_rows + p * piece, piece), :] = (
                        value * (spread_buf[at, :] * scale))

    for copy in sends:
        copy.wait_send()
    for step in range(n_dp - 1):
        for way in range(2):
            for p in range(PIECES):
                rs_copy(way, step, p).wait_send()


def on_device(n_s, n_dp, state_ensemble, predicted_data, innovations):
    rows, members = state_ensemble.shape
    count = predicted_data.shape[0]
    half = count // 2
    outers = n_s // 4
    n_sends = 4 * (n_s // 2) + 4 + 2 * (outers - 1) + 6 * (outers - 1)
    ring = (2, n_dp - 1, PIECES, rows // n_dp // 2 // PIECES, members)
    any_spec = pl.BlockSpec(memory_space=pltpu.HBM)
    return pl.pallas_call(
        functools.partial(kernel, n_s, n_dp),
        out_shape=jax.ShapeDtypeStruct((rows // n_dp, members), jnp.float32),
        in_specs=[any_spec] * 3,
        out_specs=pl.BlockSpec(memory_space=pltpu.VMEM),
        scratch_shapes=[
            pltpu.VMEM((rows, members), jnp.float32),
            pltpu.VMEM((count, members), jnp.float32),
            pltpu.VMEM((rows, members), jnp.bfloat16),
            pltpu.VMEM((rows, 1), jnp.float32),
            pltpu.VMEM((rows, members), jnp.float32),
            pltpu.VMEM((n_s, 2, members, half), jnp.bfloat16),
            pltpu.VMEM((n_s, 2, half, members), jnp.bfloat16),
            pltpu.VMEM(ring, jnp.bfloat16),
            pltpu.VMEM(ring, jnp.bfloat16),
            pltpu.SemaphoreType.DMA((5,)),
            pltpu.SemaphoreType.DMA((n_sends,)),
            pltpu.SemaphoreType.DMA((2, n_s, 2)),
            pltpu.SemaphoreType.DMA(ring[:3]),
            pltpu.SemaphoreType.DMA(ring[:3]),
        ],
        compiler_params=pltpu.CompilerParams(
            collective_id=0, has_side_effects=True, vmem_limit_bytes=67043328),
    )(state_ensemble, predicted_data, innovations)


def solution(mesh):
    in_specs = (P("state", None), P(("state", "dp"), None), P(("state", "dp"), None))
    out_specs = P(("state", "dp"), None)
    body = functools.partial(on_device, mesh.shape["state"], mesh.shape["dp"])
    return jax.shard_map(
        body, mesh=mesh, in_specs=in_specs, out_specs=out_specs, check_vma=False
    )
```

```python
import functools

import jax
import jax.numpy as jnp
from jax import lax
from jax.experimental import pallas as pl
from jax.experimental.pallas import tpu as pltpu
from jax.sharding import PartitionSpec as P

MESH = pl.DeviceIdType.MESH
WIDE_STEPS = 1
PIECES = 2


def standardize(values):
    members = values.shape[1]
    anomalies = values - jnp.mean(values, axis=1, keepdims=True)
    spread = jnp.sqrt(jnp.sum(anomalies * anomalies, axis=1, keepdims=True) / (members - 1) + 1e-06)
    return anomalies * (1.0 / spread), spread


def kernel(n_s, n_dp, state_in, data_in, innov_in, out_ref, state_raw, data_raw, sbuf, spread_buf,
           acc, dbuf, nbuf, rs_out, rs_in, local_sem, send_sem, recv_sem, rs_send_sem, rs_recv_sem):
    s = lax.axis_index("state")
    d = lax.axis_index("dp")
    rows, members = state_in.shape
    count = data_in.shape[0]
    half = count // 2
    outers = n_s // 4
    core, inner, outer = lax.rem(s, 2), lax.rem(lax.div(s, 2), 2), lax.div(s, 4)
    sib = s + 1 - 2 * core
    across = s + 2 - 4 * inner
    across_sib = sib + 2 - 4 * inner

    def other(base, k):
        return lax.rem(base + 4 * k, n_s)

    right, left = lax.rem(d + 1, n_dp), lax.rem(d + n_dp - 1, n_dp)

    load_data = [
        pltpu.make_async_copy(
            data_in.at[pl.ds(h * half, half)], data_raw.at[pl.ds(h * half, half)], local_sem.at[h])
        for h in range(2)
    ]
    load_innov = [
        pltpu.make_async_copy(
            innov_in.at[pl.ds(h * half, half)], nbuf.at[s, h], local_sem.at[2 + h])
        for h in range(2)
    ]
    load_state = pltpu.make_async_copy(state_in, state_raw, local_sem.at[4])
    for h in (1, 0):
        load_data[h].start()
    load_state.start()
    for h in range(2):
        load_innov[h].start()

    barrier = pltpu.get_barrier_semaphore()
    partners = [sib, across] + [other(s, k) for k in range(1, outers)]
    for p in partners:
        pl.semaphore_signal(barrier, inc=1, device_id={"state": p}, device_id_type=MESH)
    for p in (right, left):
        pl.semaphore_signal(barrier, inc=1, device_id={"dp": p}, device_id_type=MESH)
    pl.semaphore_wait(barrier, len(partners) + 2)

    sends = []

    def send(array, owner, h, dest, src=None):
        buf = (dbuf, nbuf)[array]
        copy = pltpu.make_async_remote_copy(
            src_ref=buf.at[owner, h] if src is None else src,
            dst_ref=buf.at[owner, h],
            send_sem=send_sem.at[len(sends)],
            recv_sem=recv_sem.at[array, owner, h],
            device_id={"state": dest},
            device_id_type=MESH,
        )
        copy.start()
        sends.append(copy)

    def arrived(array, owner, h):
        buf = (dbuf, nbuf)[array]
        pltpu.make_async_remote_copy(
            src_ref=buf.at[owner, h],
            dst_ref=buf.at[owner, h],
            send_sem=send_sem.at[0],
            recv_sem=recv_sem.at[array, owner, h],
            device_id={"state": across},
            device_id_type=MESH,
        ).wait_recv()

    outer_ks = list(range(1, outers))

    def send_innov(h, dests):
        for dest in dests:
            send(1, s, h, dest, src=innov_in.at[pl.ds(h * half, half)])

    outer_devs = [other(s, k) for k in outer_ks]
    send_innov(1, [across])
    send_innov(0, outer_devs + [sib])

    for h in (1, 0):
        load_data[h].wait()
        std, _ = standardize(data_raw[pl.ds(h * half, half), :])
        dbuf[s, h] = std.T.astype(jnp.bfloat16)
    send(0, s, 1, across)
    for dest in outer_devs:
        send(0, s, 0, dest)
    send(0, s, 0, sib)
    send_innov(0, [across])
    send_innov(1, outer_devs + [sib])
    send(0, s, 0, across)
    for dest in outer_devs:
        send(0, s, 1, dest)
    send(0, s, 1, sib)

    load_state.wait()
    tile = rows // 8
    wide = rows // WIDE_STEPS

    def state_tile(j, carry):
        at = pl.ds(pl.multiple_of(j * tile, tile), tile)
        std, spread = standardize(state_raw[at, :])
        sbuf[at, :] = std.astype(jnp.bfloat16)
        spread_buf[at, :] = spread
        return carry

    lax.fori_loop(0, 8, state_tile, 0)

    def partial(x, units):
        total = None
        for owner, h in units:
            correl = jnp.dot(x, dbuf[owner, h], preferred_element_type=jnp.float32)
            localized = (correl * correl * correl).astype(jnp.bfloat16)
            term = jnp.dot(localized, nbuf[owner, h], preferred_element_type=jnp.float32)
            total = term if total is None else total + term
        return total

    def compute(units, first=False):
        def step(j, carry):
            at = pl.ds(pl.multiple_of(j * wide, wide), wide)
            total = partial(sbuf[at, :], units)
            acc[at, :] = total if first else acc[at, :] + total
            return carry

        lax.fori_loop(0, WIDE_STEPS, step, 0)

    def both(owner, h):
        arrived(1, owner, h)
        arrived(0, owner, h)

    def take(owner, h, onward):
        for array in (1, 0):
            arrived(array, owner, h)
            for dest in onward:
                send(array, owner, h, dest)

    for h in range(2):
        load_innov[h].wait()
    compute([(s, 0), (s, 1)], first=True)
    both(sib, 0)
    both(sib, 1)
    compute([(sib, 0), (sib, 1)])

    take(across, 1, outer_devs + [sib])
    for k in outer_ks:
        take(other(s, k), 0, [across, sib])
    compute([(across, 1)] + [(other(s, k), 0) for k in outer_ks])
    both(across_sib, 1)
    for k in outer_ks:
        both(other(sib, k), 0)
    take(across, 0, [sib])
    for k in outer_ks:
        take(other(s, k), 1, [sib])
    compute([(across_sib, 1)] + [(other(sib, k), 0) for k in outer_ks])
    compute([(across, 0)] + [(other(s, k), 1) for k in outer_ks])
    both(across_sib, 0)
    for k in outer_ks:
        both(other(sib, k), 1)
    compute([(across_sib, 0)] + [(other(sib, k), 1) for k in outer_ks])

    last_units = []
    for k in outer_ks:
        own_plane, sib_plane = other(across, k), other(across_sib, k)
        for h in range(2):
            take(own_plane, h, [sib])
        if k < outers - 1:
            compute([(own_plane, 0), (own_plane, 1)])
        if k < outers - 1:
            for h in range(2):
                both(sib_plane, h)
            compute([(sib_plane, 0), (sib_plane, 1)])
        else:
            last_units = [[(own_plane, 0), (own_plane, 1)], [(sib_plane, 0), (sib_plane, 1)]]

    target_rows = rows // n_dp
    ring_rows = target_rows // 2
    piece = ring_rows // PIECES
    scale = 1.0 / float(members - 1) ** 3

    def rs_copy(way, step, p):
        return pltpu.make_async_remote_copy(
            src_ref=rs_out.at[way, step, p],
            dst_ref=rs_in.at[way, step, p],
            send_sem=rs_send_sem.at[way, step, p],
            recv_sem=rs_recv_sem.at[way, step, p],
            device_id={"dp": (right, left)[way]},
            device_id_type=MESH,
        )

    for step in range(n_dp):
        ats = []
        for way in range(2):
            target = lax.rem(d + (n_dp - 1 - step if way == 0 else 1 + step), n_dp)
            base = target * target_rows + way * ring_rows
            ats.append(pl.ds(pl.multiple_of(base, ring_rows), ring_rows))
        x = jnp.concatenate([sbuf[at, :] for at in ats], axis=0)
        if step == 0:
            total = partial(x, last_units[0])
            for owner, h in last_units[1]:
                both(owner, h)
            total = total + partial(x, last_units[1])
        else:
            total = partial(x, last_units[0] + last_units[1])
        for way in range(2):
            acc[ats[way], :] += total[way * ring_rows:(way + 1) * ring_rows]
        for p in range(PIECES):
            for way in range(2):
                target = lax.rem(d + (n_dp - 1 - step if way == 0 else 1 + step), n_dp)
                base = target * target_rows + way * ring_rows + p * piece
                at = pl.ds(pl.multiple_of(base, piece), piece)
                value = acc[at, :]
                if step > 0:
                    rs_copy(way, step - 1, p).wait_recv()
                    value = value + rs_in[way, step - 1, p].astype(jnp.float32)
                if step < n_dp - 1:
                    rs_out[way, step, p] = value.astype(jnp.bfloat16)
                    rs_copy(way, step, p).start()
                else:
                    out_ref[pl.ds(way * ring_rows + p * piece, piece), :] = (
                        value * (spread_buf[at, :] * scale))

    for copy in sends:
        copy.wait_send()
    for step in range(n_dp - 1):
        for way in range(2):
            for p in range(PIECES):
                rs_copy(way, step, p).wait_send()


def on_device(n_s, n_dp, state_ensemble, predicted_data, innovations):
    rows, members = state_ensemble.shape
    count = predicted_data.shape[0]
    half = count // 2
    outers = n_s // 4
    n_sends = 4 * (n_s // 2) + 4 + 2 * (outers - 1) + 6 * (outers - 1)
    ring = (2, n_dp - 1, PIECES, rows // n_dp // 2 // PIECES, members)
    any_spec = pl.BlockSpec(memory_space=pltpu.HBM)
    return pl.pallas_call(
        functools.partial(kernel, n_s, n_dp),
        out_shape=jax.ShapeDtypeStruct((rows // n_dp, members), jnp.float32),
        in_specs=[any_spec] * 3,
        out_specs=pl.BlockSpec(memory_space=pltpu.VMEM),
        scratch_shapes=[
            pltpu.VMEM((rows, members), jnp.float32),
            pltpu.VMEM((count, members), jnp.float32),
            pltpu.VMEM((rows, members), jnp.bfloat16),
            pltpu.VMEM((rows, 1), jnp.float32),
            pltpu.VMEM((rows, members), jnp.float32),
            pltpu.VMEM((n_s, 2, members, half), jnp.bfloat16),
            pltpu.VMEM((n_s, 2, half, members), jnp.bfloat16),
            pltpu.VMEM(ring, jnp.bfloat16),
            pltpu.VMEM(ring, jnp.bfloat16),
            pltpu.SemaphoreType.DMA((5,)),
            pltpu.SemaphoreType.DMA((n_sends,)),
            pltpu.SemaphoreType.DMA((2, n_s, 2)),
            pltpu.SemaphoreType.DMA(ring[:3]),
            pltpu.SemaphoreType.DMA(ring[:3]),
        ],
        compiler_params=pltpu.CompilerParams(
            collective_id=0, has_side_effects=True, vmem_limit_bytes=40000000),
    )(*[pltpu.with_memory_space_constraint(x, pltpu.HBM) for x in (state_ensemble, predicted_data, innovations)])


def solution(mesh):
    in_specs = (P("state", None), P(("state", "dp"), None), P(("state", "dp"), None))
    out_specs = P(("state", "dp"), None)
    body = functools.partial(on_device, mesh.shape["state"], mesh.shape["dp"])
    return jax.shard_map(
        body, mesh=mesh, in_specs=in_specs, out_specs=out_specs, check_vma=False
    )
```

```python
import functools

import jax
import jax.numpy as jnp
from jax import lax
from jax.experimental import pallas as pl
from jax.experimental.pallas import tpu as pltpu
from jax.sharding import PartitionSpec as P

MESH = pl.DeviceIdType.MESH
WIDE_STEPS = 1
PIECES = 2


def standardize(values):
    members = values.shape[1]
    anomalies = values - jnp.mean(values, axis=1, keepdims=True)
    spread = jnp.sqrt(jnp.sum(anomalies * anomalies, axis=1, keepdims=True) / (members - 1) + 1e-06)
    return anomalies * (1.0 / spread), spread


def kernel(n_s, n_dp, state_in, data_in, innov_in, out_ref, state_raw, data_raw, sbuf, spread_buf,
           acc, dbuf, nbuf, rs_out, rs_in, local_sem, send_sem, recv_sem, rs_send_sem, rs_recv_sem):
    s = lax.axis_index("state")
    d = lax.axis_index("dp")
    rows, members = state_in.shape
    count = data_in.shape[0]
    half = count // 2
    outers = n_s // 4
    core, inner, outer = lax.rem(s, 2), lax.rem(lax.div(s, 2), 2), lax.div(s, 4)
    sib = s + 1 - 2 * core
    across = s + 2 - 4 * inner
    across_sib = sib + 2 - 4 * inner

    def other(base, k):
        return lax.rem(base + 4 * k, n_s)

    right, left = lax.rem(d + 1, n_dp), lax.rem(d + n_dp - 1, n_dp)

    load_data = [
        pltpu.make_async_copy(
            data_in.at[pl.ds(h * half, half)], data_raw.at[pl.ds(h * half, half)], local_sem.at[h])
        for h in range(2)
    ]
    load_innov = [
        pltpu.make_async_copy(
            innov_in.at[pl.ds(h * half, half)], nbuf.at[s, h], local_sem.at[2 + h])
        for h in range(2)
    ]
    load_state = pltpu.make_async_copy(state_in, state_raw, local_sem.at[4])
    for h in (1, 0):
        load_data[h].start()
    load_state.start()
    for h in range(2):
        load_innov[h].start()

    barrier = pltpu.get_barrier_semaphore()
    partners = [sib, across] + [other(s, k) for k in range(1, outers)]
    for p in partners:
        pl.semaphore_signal(barrier, inc=1, device_id={"state": p}, device_id_type=MESH)
    for p in (right, left):
        pl.semaphore_signal(barrier, inc=1, device_id={"dp": p}, device_id_type=MESH)
    pl.semaphore_wait(barrier, len(partners) + 2)

    sends = []

    def send(array, owner, h, dest, src=None):
        buf = (dbuf, nbuf)[array]
        copy = pltpu.make_async_remote_copy(
            src_ref=buf.at[owner, h] if src is None else src,
            dst_ref=buf.at[owner, h],
            send_sem=send_sem.at[len(sends)],
            recv_sem=recv_sem.at[array, owner, h],
            device_id={"state": dest},
            device_id_type=MESH,
        )
        copy.start()
        sends.append(copy)

    def arrived(array, owner, h):
        buf = (dbuf, nbuf)[array]
        pltpu.make_async_remote_copy(
            src_ref=buf.at[owner, h],
            dst_ref=buf.at[owner, h],
            send_sem=send_sem.at[0],
            recv_sem=recv_sem.at[array, owner, h],
            device_id={"state": across},
            device_id_type=MESH,
        ).wait_recv()

    outer_ks = list(range(1, outers))

    def send_innov(h, dests):
        for dest in dests:
            send(1, s, h, dest, src=innov_in.at[pl.ds(h * half, half)])

    outer_devs = [other(s, k) for k in outer_ks]
    send_innov(1, [across])
    send_innov(0, outer_devs + [sib])

    for h in (1, 0):
        load_data[h].wait()
        std, _ = standardize(data_raw[pl.ds(h * half, half), :])
        dbuf[s, h] = std.T.astype(jnp.bfloat16)
    send(0, s, 1, across)
    for dest in outer_devs:
        send(0, s, 0, dest)
    send(0, s, 0, sib)
    send_innov(0, [across])
    send_innov(1, outer_devs + [sib])
    send(0, s, 0, across)
    for dest in outer_devs:
        send(0, s, 1, dest)
    send(0, s, 1, sib)

    load_state.wait()
    tile = rows // 8
    wide = rows // WIDE_STEPS

    def state_tile(j, carry):
        at = pl.ds(pl.multiple_of(j * tile, tile), tile)
        std, spread = standardize(state_raw[at, :])
        sbuf[at, :] = std.astype(jnp.bfloat16)
        spread_buf[at, :] = spread
        return carry

    lax.fori_loop(0, 8, state_tile, 0)

    def partial(x, units):
        total = None
        for owner, h in units:
            correl = jnp.dot(x, dbuf[owner, h], preferred_element_type=jnp.float32)
            localized = (correl * correl * correl).astype(jnp.bfloat16)
            term = jnp.dot(localized, nbuf[owner, h], preferred_element_type=jnp.float32)
            total = term if total is None else total + term
        return total

    def compute(units, first=False):
        def step(j, carry):
            at = pl.ds(pl.multiple_of(j * wide, wide), wide)
            total = partial(sbuf[at, :], units)
            acc[at, :] = total if first else acc[at, :] + total
            return carry

        lax.fori_loop(0, WIDE_STEPS, step, 0)

    def both(owner, h):
        arrived(1, owner, h)
        arrived(0, owner, h)

    def take(owner, h, onward):
        for array in (1, 0):
            arrived(array, owner, h)
            for dest in onward:
                send(array, owner, h, dest)

    for h in range(2):
        load_innov[h].wait()
    compute([(s, 0), (s, 1)], first=True)
    both(sib, 0)
    both(sib, 1)
    compute([(sib, 0), (sib, 1)])

    take(across, 1, outer_devs + [sib])
    for k in outer_ks:
        take(other(s, k), 0, [across, sib])
    compute([(across, 1)] + [(other(s, k), 0) for k in outer_ks])
    both(across_sib, 1)
    for k in outer_ks:
        both(other(sib, k), 0)
    take(across, 0, [sib])
    for k in outer_ks:
        take(other(s, k), 1, [sib])
    compute([(across_sib, 1)] + [(other(sib, k), 0) for k in outer_ks])
    compute([(across, 0)] + [(other(s, k), 1) for k in outer_ks])
    both(across_sib, 0)
    for k in outer_ks:
        both(other(sib, k), 1)
    compute([(across_sib, 0)] + [(other(sib, k), 1) for k in outer_ks])

    last_units = []
    for k in outer_ks:
        own_plane, sib_plane = other(across, k), other(across_sib, k)
        for h in range(2):
            take(own_plane, h, [sib])
        if k < outers - 1:
            compute([(own_plane, 0), (own_plane, 1)])
        if k < outers - 1:
            for h in range(2):
                both(sib_plane, h)
            compute([(sib_plane, 0), (sib_plane, 1)])
        else:
            last_units = [[(own_plane, 0), (own_plane, 1)], [(sib_plane, 0), (sib_plane, 1)]]

    target_rows = rows // n_dp
    ring_rows = target_rows // 2
    piece = ring_rows // PIECES
    scale = 1.0 / float(members - 1) ** 3

    def rs_copy(way, step, p):
        return pltpu.make_async_remote_copy(
            src_ref=rs_out.at[way, step, p],
            dst_ref=rs_in.at[way, step, p],
            send_sem=rs_send_sem.at[way, step, p],
            recv_sem=rs_recv_sem.at[way, step, p],
            device_id={"dp": (right, left)[way]},
            device_id_type=MESH,
        )

    def ring_at(way, step, first, size):
        target = lax.rem(d + (n_dp - 1 - step if way == 0 else 1 + step), n_dp)
        base = target * target_rows + way * ring_rows + first
        return pl.ds(pl.multiple_of(base, size), size)

    def last_blocks(step, first, size):
        ats = [ring_at(way, step, first, size) for way in range(2)]
        x = jnp.concatenate([sbuf[at, :] for at in ats], axis=0)
        if step == 0:
            total = partial(x, last_units[0])
            if first == 0:
                for owner, h in last_units[1]:
                    both(owner, h)
            total = total + partial(x, last_units[1])
        else:
            total = partial(x, last_units[0] + last_units[1])
        for way in range(2):
            acc[ats[way], :] += total[way * size:(way + 1) * size]

    for step in range(n_dp):
        if step > 0:
            last_blocks(step, 0, ring_rows)
        for p in range(PIECES):
            if step == 0:
                last_blocks(step, p * piece, piece)
            for way in range(2):
                at = ring_at(way, step, p * piece, piece)
                value = acc[at, :]
                if step > 0:
                    rs_copy(way, step - 1, p).wait_recv()
                    value = value + rs_in[way, step - 1, p].astype(jnp.float32)
                if step < n_dp - 1:
                    rs_out[way, step, p] = value.astype(jnp.bfloat16)
                    rs_copy(way, step, p).start()
                else:
                    out_ref[pl.ds(way * ring_rows + p * piece, piece), :] = (
                        value * (spread_buf[at, :] * scale))

    for copy in sends:
        copy.wait_send()
    for step in range(n_dp - 1):
        for way in range(2):
            for p in range(PIECES):
                rs_copy(way, step, p).wait_send()


def on_device(n_s, n_dp, state_ensemble, predicted_data, innovations):
    rows, members = state_ensemble.shape
    count = predicted_data.shape[0]
    half = count // 2
    outers = n_s // 4
    n_sends = 4 * (n_s // 2) + 4 + 2 * (outers - 1) + 6 * (outers - 1)
    ring = (2, n_dp - 1, PIECES, rows // n_dp // 2 // PIECES, members)
    any_spec = pl.BlockSpec(memory_space=pltpu.HBM)
    return pl.pallas_call(
        functools.partial(kernel, n_s, n_dp),
        out_shape=jax.ShapeDtypeStruct((rows // n_dp, members), jnp.float32),
        in_specs=[any_spec] * 3,
        out_specs=pl.BlockSpec(memory_space=pltpu.VMEM),
        scratch_shapes=[
            pltpu.VMEM((rows, members), jnp.float32),
            pltpu.VMEM((count, members), jnp.float32),
            pltpu.VMEM((rows, members), jnp.bfloat16),
            pltpu.VMEM((rows, 1), jnp.float32),
            pltpu.VMEM((rows, members), jnp.float32),
            pltpu.VMEM((n_s, 2, members, half), jnp.bfloat16),
            pltpu.VMEM((n_s, 2, half, members), jnp.bfloat16),
            pltpu.VMEM(ring, jnp.bfloat16),
            pltpu.VMEM(ring, jnp.bfloat16),
            pltpu.SemaphoreType.DMA((5,)),
            pltpu.SemaphoreType.DMA((n_sends,)),
            pltpu.SemaphoreType.DMA((2, n_s, 2)),
            pltpu.SemaphoreType.DMA(ring[:3]),
            pltpu.SemaphoreType.DMA(ring[:3]),
        ],
        compiler_params=pltpu.CompilerParams(
            collective_id=0, has_side_effects=True, vmem_limit_bytes=40000000),
    )(*[pltpu.with_memory_space_constraint(x, pltpu.HBM) for x in (state_ensemble, predicted_data, innovations)])


def solution(mesh):
    in_specs = (P("state", None), P(("state", "dp"), None), P(("state", "dp"), None))
    out_specs = P(("state", "dp"), None)
    body = functools.partial(on_device, mesh.shape["state"], mesh.shape["dp"])
    return jax.shard_map(
        body, mesh=mesh, in_specs=in_specs, out_specs=out_specs, check_vma=False
    )
```
